32 devices in a mesh: rep: 4 (over x, core), shard: 8 (over z, y).
Axes of the slice: x: 2, y: 2, z: 4, core: 2. Of those that a mesh axis runs over, the one named last changes fastest.
Arguments:
- block_input: float32 [32, 256, 768], P(('rep', 'shard')), may hold values from -6 to 6
- attn_gain: bfloat16 [768], P('shard'), may hold values from 0.099609375 to 1.8984375
- attn_shift: bfloat16 [768], P('shard'), may hold values from -3 to 3
- query_weight: bfloat16 [768, 768], P('shard'), may hold values from -4 to 4
- query_bias: bfloat16 [768], P('shard'), may hold values from -3 to 3
- key_weight: bfloat16 [768, 768], P('shard'), may hold values from -4 to 4
- value_weight: bfloat16 [768, 768], P('shard'), may hold values from -0.21875 to 0.21875
- value_bias: bfloat16 [768], P('shard'), may hold values from -0.3125 to 0.3125
- out_weight: bfloat16 [768, 768], P('shard'), may hold values from -3.5 to 3.5
- out_bias: bfloat16 [768], P('shard'), may hold values from -3 to 3
- mlp_gain: bfloat16 [768], P('shard'), may hold values from 0.099609375 to 1.8984375
- mlp_shift: bfloat16 [768], P('shard'), may hold values from -3 to 3
- hidden_weight: bfloat16 [768, 3072], P('shard'), may hold values from -0.21875 to 0.21875
- hidden_bias: bfloat16 [3072], P('shard'), may hold values from -3 to 3
- proj_weight: bfloat16 [3072, 768], P('shard'), may hold values from -0.109375 to 0.109375
- proj_bias: bfloat16 [768], P('shard'), may hold values from -3 to 3
- out_cotangent: float32 [32, 256, 768], P(('rep', 'shard')), may hold values from -6 to 6
Outputs:
- block_output: float32 [32, 256, 768], P(('rep', 'shard'))
- input_grad: float32 [32, 256, 768], P(('rep', 'shard'))
- attn_gain_grad: float32 [768], P('shard')
- attn_shift_grad: float32 [768], P('shard')
- query_weight_grad: float32 [768, 768], P('shard')
- query_bias_grad: float32 [768], P('shard')
- key_weight_grad: float32 [768, 768], P('shard')
- value_weight_grad: float32 [768, 768], P('shard')
- value_bias_grad: float32 [768], P('shard')
- out_weight_grad: float32 [768, 768], P('shard')
- out_bias_grad: float32 [768], P('shard')
- mlp_gain_grad: float32 [768], P('shard')
- mlp_shift_grad: float32 [768], P('shard')
- hidden_weight_grad: float32 [768, 3072], P('shard')
- hidden_bias_grad: float32 [3072], P('shard')
- proj_weight_grad: float32 [3072, 768], P('shard')
- proj_bias_grad: float32 [768], P('shard')
The draws below stay inside these ranges and needn't reach their ends.
All inputs are finite; a program needn't handle non-finite values.
Results may differ from the reference program's by a relative error of at most 0.02.
The reference program's roundings to bfloat16 on the way count: a program that leaves them out, or rounds other values in their place, can miss the bound.
Values may be sent and summed in bfloat16 or wider, within the bound.
A program may use at most 128 MiB of HBM per device.

```python
import math
import jax
import jax.numpy as jnp
from jax import lax

D = 768
HD = 64
FF = 3072
CLIP = 256
CLIPS = 32


def draw_query_weight(key, part):
    own = jax.random.truncated_normal(jax.random.fold_in(key, 1), -4.0, 4.0, (D, D), jnp.float32) * D ** (-0.5)
    return own.astype(jnp.bfloat16)


def draw_key_weight(key, part):
    own = jax.random.truncated_normal(jax.random.fold_in(key, 2), -4.0, 4.0, (D, D), jnp.float32) * D ** (-0.5)
    return own.astype(jnp.bfloat16)


def block_levels(key, shape, cuts, smallest, largest):
    level = 1.0
    for axis_at, shards_of in cuts:
        heights = jax.random.uniform(jax.random.fold_in(jax.random.fold_in(key, 6), axis_at), (shards_of,), jnp.float32, smallest / len(cuts), largest / len(cuts))
        level = level * jnp.repeat(jnp.exp(heights), shape[axis_at] // shards_of).reshape((-1,) + (1,) * (len(shape) - 1 - axis_at))
    return level


def noise(own_key, dims, width, reach, pieces=(), kind=jnp.bfloat16):
    level = block_levels(own_key, dims, pieces, -0.22, 0.18) if pieces else 1.0
    array = jax.random.normal(own_key, dims, jnp.float32) * width * level
    return jnp.minimum(jnp.maximum(array, -reach), reach).astype(kind)


def setup_inputs(seed: int = 0) -> dict:
    key_of = jax.random.split(jax.random.key(seed), 18)
    return {
        "block_input": noise(key_of[0], (CLIPS, CLIP, D), 1.0, 6.0, ((0, 32),), jnp.float32),
        "attn_gain": jnp.clip(1.0 + 0.18 * jax.random.normal(key_of[1], (D,), jnp.float32), 0.099609375, 1.8984375).astype(jnp.bfloat16),
        "attn_shift": noise(key_of[2], (D,), 0.5, 3.0, ((0, 8),)),
        "query_weight": draw_query_weight(jax.random.fold_in(key_of[17], 71), 0),
        "query_bias": noise(key_of[4], (D,), 0.5, 3.0, ((0, 8),)),
        "key_weight": draw_key_weight(jax.random.fold_in(key_of[17], 71), 0),
        "value_weight": noise(key_of[6], (D, D), D ** -0.5, 0.21875, ((0, 8),)),
        "value_bias": noise(key_of[7], (D,), 0.02, 0.3125, ((0, 8),)),
        "out_weight": noise(key_of[8], (D, D), (max(D // CLIP, 1)) ** -0.5, 3.5, ((0, 8),)),
        "out_bias": noise(key_of[9], (D,), 0.5, 3.0, ((0, 8),)),
        "mlp_gain": jnp.clip(1.0 + 0.18 * jax.random.normal(key_of[10], (D,), jnp.float32), 0.099609375, 1.8984375).astype(jnp.bfloat16),
        "mlp_shift": noise(key_of[11], (D,), 0.5, 3.0, ((0, 8),)),
        "hidden_weight": noise(key_of[12], (D, FF), D ** -0.5, 0.21875, ((0, 8),)),
        "hidden_bias": noise(key_of[13], (FF,), 0.5, 3.0, ((0, 8),)),
        "proj_weight": noise(key_of[14], (FF, D), FF ** -0.5, 0.109375, ((0, 8),)),
        "proj_bias": noise(key_of[15], (D,), 0.5, 3.0, ((0, 8),)),
        "out_cotangent": noise(key_of[16], (CLIPS, CLIP, D), 1.0, 6.0, ((0, 32),), jnp.float32),
    }


EPS = 1e-05
ROOT_HALF = 0.7071067811865476
INV_ROOT_TWO_PI = 0.3989422804014327

def layer_norm(tokens, norm_gain, norm_shift):
    average = lax.optimization_barrier(jnp.mean(tokens, axis=-1, keepdims=True))
    centered = tokens - average
    inv_std = lax.rsqrt(lax.optimization_barrier(jnp.mean(centered * centered, axis=-1, keepdims=True)) + EPS)
    normed = centered * inv_std
    shaped = normed * norm_gain.astype(jnp.float32) + norm_shift.astype(jnp.float32)
    return (normed, inv_std, shaped.astype(jnp.bfloat16))

def norm_grad(upstream, normed, inv_std, norm_gain):
    scaled = upstream * norm_gain.astype(jnp.float32)
    inner = scaled - lax.optimization_barrier(jnp.mean(scaled, axis=-1, keepdims=True)) - normed * lax.optimization_barrier(jnp.mean(scaled * normed, axis=-1, keepdims=True))
    return (inner * inv_std, lax.optimization_barrier(jnp.sum(upstream * normed, axis=0)), lax.optimization_barrier(jnp.sum(upstream, axis=0)))

def matmul(left, right):
    return jnp.dot(left, right, preferred_element_type=jnp.float32)

def times_transposed(left, right):
    return jnp.dot(left, right.T, preferred_element_type=jnp.float32)

def token_sum(left, right):
    return jnp.dot(left.T, right, preferred_element_type=jnp.float32)

def gelu_parts(before):
    normal_cdf = 0.5 * (1.0 + lax.erf(before * ROOT_HALF))
    return (before * normal_cdf, normal_cdf + before * INV_ROOT_TWO_PI * jnp.exp(-0.5 * before * before))

def widen(tensor):
    return tensor.astype(jnp.float32)

def attend(query, keys, values):
    factor = query.shape[-1] ** (-0.5)
    scores = jnp.einsum('clhd,cmhd->chlm', widen(query), widen(keys)) * factor
    row_top = lax.optimization_barrier(jnp.max(scores, axis=-1, keepdims=True))
    log_total = row_top + jnp.log(lax.optimization_barrier(jnp.sum(jnp.exp(scores - row_top), axis=-1, keepdims=True)))
    weights = jnp.exp(scores - log_total).astype(jnp.bfloat16)
    mixed = jnp.einsum('chlm,cmhd->clhd', widen(weights), widen(values)).astype(jnp.bfloat16)
    return (mixed, log_total)

def attend_grad(query, keys, values, mixed, log_total, grad_mixed):
    factor = query.shape[-1] ** (-0.5)
    scores = jnp.einsum('clhd,cmhd->chlm', widen(query), widen(keys)) * factor
    weights = jnp.exp(scores - log_total)
    weights_low = weights.astype(jnp.bfloat16)
    grad_values = jnp.einsum('chlm,clhd->cmhd', widen(weights_low), widen(grad_mixed))
    grad_weights = jnp.einsum('clhd,cmhd->chlm', widen(grad_mixed), widen(values))
    delta = lax.optimization_barrier(jnp.sum(widen(grad_mixed) * widen(mixed), axis=-1))
    delta = jnp.transpose(delta, (0, 2, 1))[..., None]
    grad_scores = (weights * (grad_weights - delta)).astype(jnp.bfloat16)
    grad_query = jnp.einsum('chlm,cmhd->clhd', widen(grad_scores), widen(keys)) * factor
    grad_keys = jnp.einsum('chlm,clhd->cmhd', widen(grad_scores), widen(query)) * factor
    return (grad_query, grad_keys, grad_values)

def block_pass(params, inputs, cotangent):
    attn_gain, attn_shift, query_weight, query_bias, key_weight, value_weight, value_bias, out_weight, out_bias, mlp_gain, mlp_shift, hidden_weight, hidden_bias, proj_weight, proj_bias = params
    clip_count, frame_count, model_width = inputs.shape
    head_count = model_width // HD
    token_count = clip_count * frame_count

    def split_heads(matrix):
        return matrix.reshape(clip_count, frame_count, head_count, HD)

    def join_heads(tensor):
        return tensor.reshape(token_count, model_width)
    residual = inputs.reshape(token_count, model_width)
    normed_one, inv_one, input_low = layer_norm(residual, attn_gain, attn_shift)
    query_low = (matmul(input_low, query_weight) + query_bias.astype(jnp.float32)).astype(jnp.bfloat16)
    keys_low = matmul(input_low, key_weight).astype(jnp.bfloat16)
    values_low = (matmul(input_low, value_weight) + value_bias.astype(jnp.float32)).astype(jnp.bfloat16)
    mixed, log_total = attend(split_heads(query_low), split_heads(keys_low), split_heads(values_low))
    mixed_rows = join_heads(mixed)
    middle = residual + matmul(mixed_rows, out_weight) + out_bias.astype(jnp.float32)
    normed_two, inv_two, middle_low = layer_norm(middle, mlp_gain, mlp_shift)
    before_act = matmul(middle_low, hidden_weight) + hidden_bias.astype(jnp.float32)
    activated, slope = gelu_parts(before_act)
    act_low = activated.astype(jnp.bfloat16)
    block_output = middle + matmul(act_low, proj_weight) + proj_bias.astype(jnp.float32)
    upstream = cotangent.reshape(token_count, model_width)
    up_low = upstream.astype(jnp.bfloat16)
    proj_term = token_sum(act_low, up_low)
    proj_bias_term = lax.optimization_barrier(jnp.sum(upstream, axis=0))
    grad_before = times_transposed(up_low, proj_weight) * slope
    before_low = grad_before.astype(jnp.bfloat16)
    hidden_term = token_sum(middle_low, before_low)
    hidden_bias_term = lax.optimization_barrier(jnp.sum(grad_before, axis=0))
    grad_normed_two = times_transposed(before_low, hidden_weight)
    grad_middle_norm, mlp_gain_term, mlp_shift_term = norm_grad(grad_normed_two, normed_two, inv_two, mlp_gain)
    grad_middle = upstream + grad_middle_norm
    middle_grad_low = grad_middle.astype(jnp.bfloat16)
    out_term = token_sum(mixed_rows, middle_grad_low)
    out_bias_term = lax.optimization_barrier(jnp.sum(grad_middle, axis=0))
    grad_mixed = times_transposed(middle_grad_low, out_weight).astype(jnp.bfloat16)
    grad_query, grad_keys, grad_values = attend_grad(split_heads(query_low), split_heads(keys_low), split_heads(values_low), mixed, log_total, split_heads(grad_mixed))
    grad_query = join_heads(grad_query)
    grad_keys = join_heads(grad_keys)
    grad_values = join_heads(grad_values)
    query_bias_term = lax.optimization_barrier(jnp.sum(grad_query, axis=0))
    value_bias_term = lax.optimization_barrier(jnp.sum(grad_values, axis=0))
    query_grad_low = grad_query.astype(jnp.bfloat16)
    key_grad_low = grad_keys.astype(jnp.bfloat16)
    value_grad_low = grad_values.astype(jnp.bfloat16)
    query_term = token_sum(input_low, query_grad_low)
    key_term = token_sum(input_low, key_grad_low)
    value_term = token_sum(input_low, value_grad_low)
    grad_normed_one = times_transposed(query_grad_low, query_weight) + times_transposed(key_grad_low, key_weight) + times_transposed(value_grad_low, value_weight)
    grad_input_norm, attn_gain_term, attn_shift_term = norm_grad(grad_normed_one, normed_one, inv_one, attn_gain)
    input_grad = grad_middle + grad_input_norm
    grads = (attn_gain_term, attn_shift_term, query_term, query_bias_term, key_term, value_term, value_bias_term, out_term, out_bias_term, mlp_gain_term, mlp_shift_term, hidden_term, hidden_bias_term, proj_term, proj_bias_term)
    return (block_output.reshape(inputs.shape), input_grad.reshape(inputs.shape), grads)

def reference(block_input, attn_gain, attn_shift, query_weight, query_bias, key_weight, value_weight, value_bias, out_weight, out_bias, mlp_gain, mlp_shift, hidden_weight, hidden_bias, proj_weight, proj_bias, out_cotangent):
    params = (attn_gain, attn_shift, query_weight, query_bias, key_weight, value_weight, value_bias, out_weight, out_bias, mlp_gain, mlp_shift, hidden_weight, hidden_bias, proj_weight, proj_bias)
    group = math.gcd(CLIPS, max(1, 4096 // CLIP))
    block_count = CLIPS // group
    inputs_all = block_input.reshape(block_count, group, CLIP, D)
    cotangents_all = out_cotangent.reshape(block_count, group, CLIP, D)
    zeros = tuple((jnp.zeros(param.shape, jnp.float32) for param in params))

    def advance(carry, item):
        output_part, grad_part, grads = block_pass(params, item[0], item[1])
        return (tuple((left + right for left, right in zip(carry, grads))), (output_part, grad_part))
    totals, stacked = lax.scan(advance, zeros, (inputs_all, cotangents_all))
    grad_a, grad_b, grad_c, grad_d, grad_e, grad_f, grad_g, grad_h, grad_i, grad_j, grad_k, grad_l, grad_m, grad_n, grad_o = totals
    return (stacked[0].reshape(CLIPS, CLIP, D), stacked[1].reshape(CLIPS, CLIP, D), grad_a, grad_b, grad_c, grad_d, grad_e, grad_f, grad_g, grad_h, grad_i, grad_j, grad_k, grad_l, grad_m, grad_n, grad_o)
```

```python
import jax
import jax.numpy as jnp
from jax import lax
from jax.sharding import PartitionSpec as P

HD = 64


EPS = 1e-05
ROOT_HALF = 0.7071067811865476
INV_ROOT_TWO_PI = 0.3989422804014327


def layer_norm(tokens, norm_gain, norm_shift):
    average = jnp.mean(tokens, axis=-1, keepdims=True)
    centered = tokens - average
    inv_std = lax.rsqrt(jnp.mean(centered * centered, axis=-1, keepdims=True) + EPS)
    normed = centered * inv_std
    shaped = normed * norm_gain.astype(jnp.float32) + norm_shift.astype(jnp.float32)
    return (normed, inv_std, shaped.astype(jnp.bfloat16))


def norm_grad(upstream, normed, inv_std, norm_gain):
    scaled = upstream * norm_gain.astype(jnp.float32)
    inner = (
        scaled
        - jnp.mean(scaled, axis=-1, keepdims=True)
        - normed * jnp.mean(scaled * normed, axis=-1, keepdims=True)
    )
    return (inner * inv_std, jnp.sum(upstream * normed, axis=0), jnp.sum(upstream, axis=0))


def matmul(left, right):
    return jnp.dot(left, right, preferred_element_type=jnp.float32)


def times_transposed(left, right):
    return lax.dot_general(
        left, right, (((1,), (1,)), ((), ())), preferred_element_type=jnp.float32
    )


def token_sum(left, right):
    return lax.dot_general(
        left, right, (((0,), (0,)), ((), ())), preferred_element_type=jnp.float32
    )


def gelu_parts(before):
    normal_cdf = 0.5 * (1.0 + lax.erf(before * ROOT_HALF))
    return (
        before * normal_cdf,
        normal_cdf + before * INV_ROOT_TWO_PI * jnp.exp(-0.5 * before * before),
    )


def attend(query, keys, values):
    factor = query.shape[-1] ** (-0.5)
    scores = jnp.einsum("clhd,cmhd->chlm", query, keys, preferred_element_type=jnp.float32) * factor
    row_top = jnp.max(scores, axis=-1, keepdims=True)
    log_total = row_top + jnp.log(jnp.sum(jnp.exp(scores - row_top), axis=-1, keepdims=True))
    weights = jnp.exp(scores - log_total).astype(jnp.bfloat16)
    mixed = jnp.einsum(
        "chlm,cmhd->clhd", weights, values, preferred_element_type=jnp.float32
    ).astype(jnp.bfloat16)
    return (mixed, log_total)


def attend_grad(query, keys, values, mixed, log_total, grad_mixed):
    factor = query.shape[-1] ** (-0.5)
    scores = jnp.einsum("clhd,cmhd->chlm", query, keys, preferred_element_type=jnp.float32) * factor
    weights = jnp.exp(scores - log_total)
    weights_low = weights.astype(jnp.bfloat16)
    grad_values = jnp.einsum(
        "chlm,clhd->cmhd", weights_low, grad_mixed, preferred_element_type=jnp.float32
    )
    grad_weights = jnp.einsum(
        "clhd,cmhd->chlm", grad_mixed, values, preferred_element_type=jnp.float32
    )
    delta = jnp.sum(grad_mixed.astype(jnp.float32) * mixed.astype(jnp.float32), axis=-1)
    delta = jnp.transpose(delta, (0, 2, 1))[..., None]
    grad_scores = (weights * (grad_weights - delta)).astype(jnp.bfloat16)
    grad_query = (
        jnp.einsum("chlm,cmhd->clhd", grad_scores, keys, preferred_element_type=jnp.float32)
        * factor
    )
    grad_keys = (
        jnp.einsum("chlm,clhd->cmhd", grad_scores, query, preferred_element_type=jnp.float32)
        * factor
    )
    return (grad_query, grad_keys, grad_values)


def cut_columns(matrix, likes, flat=True):
    pieces = []
    start = 0
    for like in likes:
        width = like.shape[-1]
        piece = matrix[:, start : start + width]
        pieces.append(piece.reshape(-1) if flat else piece)
        start += width
    return tuple(pieces)


def on_device(
    block_input,
    attn_gain,
    attn_shift,
    query_weight,
    query_bias,
    key_weight,
    value_weight,
    value_bias,
    out_weight,
    out_bias,
    mlp_gain,
    mlp_shift,
    hidden_weight,
    hidden_bias,
    proj_weight,
    proj_bias,
    out_cotangent,
):
    clip_count, frame_count, model_width = block_input.shape
    head_count = model_width // HD
    token_count = clip_count * frame_count

    def split_heads(matrix):
        return matrix.reshape(clip_count, frame_count, head_count, HD)

    def join_heads(tensor):
        return tensor.reshape(token_count, model_width)

    residual = block_input.reshape(token_count, model_width)
    vectors = (
        attn_gain,
        attn_shift,
        query_bias,
        value_bias,
        out_bias,
        mlp_gain,
        mlp_shift,
        proj_bias,
        hidden_bias,
    )
    squares = (query_weight, key_weight, value_weight, out_weight, hidden_weight)
    vectors_all = lax.all_gather(jnp.concatenate(vectors), "shard", axis=0, tiled=False)
    squares_all = lax.all_gather(jnp.concatenate(squares, axis=1), "shard", axis=0, tiled=True)
    proj_all = lax.all_gather(proj_weight, "shard", axis=0, tiled=True)
    (
        attn_gain_all,
        attn_shift_all,
        query_bias_all,
        value_bias_all,
        out_bias_all,
        mlp_gain_all,
        mlp_shift_all,
        proj_bias_all,
        hidden_bias_all,
    ) = cut_columns(vectors_all, vectors)
    query_all, key_all, value_all, out_all, hidden_all = cut_columns(squares_all, squares, False)
    normed_one, inv_one, input_low = layer_norm(residual, attn_gain_all, attn_shift_all)
    query_low = (matmul(input_low, query_all) + query_bias_all.astype(jnp.float32)).astype(
        jnp.bfloat16
    )
    keys_low = matmul(input_low, key_all).astype(jnp.bfloat16)
    values_low = (matmul(input_low, value_all) + value_bias_all.astype(jnp.float32)).astype(
        jnp.bfloat16
    )
    mixed, log_total = attend(
        split_heads(query_low), split_heads(keys_low), split_heads(values_low)
    )
    mixed_rows = join_heads(mixed)
    middle = residual + matmul(mixed_rows, out_all) + out_bias_all.astype(jnp.float32)
    normed_two, inv_two, middle_low = layer_norm(middle, mlp_gain_all, mlp_shift_all)
    before_act = matmul(middle_low, hidden_all) + hidden_bias_all.astype(jnp.float32)
    activated, slope = gelu_parts(before_act)
    act_low = activated.astype(jnp.bfloat16)
    block_output = middle + matmul(act_low, proj_all) + proj_bias_all.astype(jnp.float32)
    upstream = out_cotangent.reshape(token_count, model_width)
    up_low = upstream.astype(jnp.bfloat16)
    proj_term = token_sum(act_low, up_low)
    proj_bias_term = jnp.sum(upstream, axis=0)
    grad_before = times_transposed(up_low, proj_all) * slope
    before_low = grad_before.astype(jnp.bfloat16)
    hidden_term = token_sum(middle_low, before_low)
    hidden_bias_term = jnp.sum(grad_before, axis=0)
    grad_normed_two = times_transposed(before_low, hidden_all)
    grad_middle_norm, mlp_gain_term, mlp_shift_term = norm_grad(
        grad_normed_two, normed_two, inv_two, mlp_gain_all
    )
    grad_middle = upstream + grad_middle_norm
    middle_grad_low = grad_middle.astype(jnp.bfloat16)
    out_term = token_sum(mixed_rows, middle_grad_low)
    out_bias_term = jnp.sum(grad_middle, axis=0)
    grad_mixed = times_transposed(middle_grad_low, out_all).astype(jnp.bfloat16)
    grad_query, grad_keys, grad_values = attend_grad(
        split_heads(query_low),
        split_heads(keys_low),
        split_heads(values_low),
        mixed,
        log_total,
        split_heads(grad_mixed),
    )
    grad_query = join_heads(grad_query)
    grad_keys = join_heads(grad_keys)
    grad_values = join_heads(grad_values)
    query_bias_term = jnp.sum(grad_query, axis=0)
    value_bias_term = jnp.sum(grad_values, axis=0)
    query_grad_low = grad_query.astype(jnp.bfloat16)
    key_grad_low = grad_keys.astype(jnp.bfloat16)
    value_grad_low = grad_values.astype(jnp.bfloat16)
    query_term = token_sum(input_low, query_grad_low)
    key_term = token_sum(input_low, key_grad_low)
    value_term = token_sum(input_low, value_grad_low)
    grad_normed_one = (
        times_transposed(query_grad_low, query_all)
        + times_transposed(key_grad_low, key_all)
        + times_transposed(value_grad_low, value_all)
    )
    grad_input_norm, attn_gain_term, attn_shift_term = norm_grad(
        grad_normed_one, normed_one, inv_one, attn_gain_all
    )
    input_grad = grad_middle + grad_input_norm
    shards = lax.axis_size("shard")
    vector_terms = jnp.concatenate(
        [
            term.reshape(shards, -1)
            for term in (
                attn_gain_term,
                attn_shift_term,
                query_bias_term,
                value_bias_term,
                out_bias_term,
                mlp_gain_term,
                mlp_shift_term,
                proj_bias_term,
                hidden_bias_term,
            )
        ],
        axis=1,
    )
    square_terms = jnp.concatenate(
        [
            term.astype(jnp.bfloat16)
            for term in (query_term, key_term, value_term, out_term, hidden_term)
        ],
        axis=1,
    )
    vector_owned = lax.psum(vector_terms, ("rep", "shard"))
    vector_owned = lax.dynamic_index_in_dim(
        vector_owned, lax.axis_index("shard"), 0, keepdims=False
    )
    square_owned = lax.psum_scatter(square_terms, "shard", scatter_dimension=0, tiled=True)
    proj_owned = lax.psum_scatter(
        proj_term.astype(jnp.bfloat16), "shard", scatter_dimension=0, tiled=True
    )
    square_owned = lax.psum(square_owned, "rep").astype(jnp.float32)
    proj_weight_grad = lax.psum(proj_owned, "rep").astype(jnp.float32)
    (
        attn_gain_grad,
        attn_shift_grad,
        query_bias_grad,
        value_bias_grad,
        out_bias_grad,
        mlp_gain_grad,
        mlp_shift_grad,
        proj_bias_grad,
        hidden_bias_grad,
    ) = cut_columns(vector_owned[None, :], vectors)
    (
        query_weight_grad,
        key_weight_grad,
        value_weight_grad,
        out_weight_grad,
        hidden_weight_grad,
    ) = cut_columns(square_owned, squares, False)
    return (
        block_output.reshape(clip_count, frame_count, model_width),
        input_grad.reshape(clip_count, frame_count, model_width),
        attn_gain_grad,
        attn_shift_grad,
        query_weight_grad,
        query_bias_grad,
        key_weight_grad,
        value_weight_grad,
        value_bias_grad,
        out_weight_grad,
        out_bias_grad,
        mlp_gain_grad,
        mlp_shift_grad,
        hidden_weight_grad,
        hidden_bias_grad,
        proj_weight_grad,
        proj_bias_grad,
    )


def solution(mesh):
    placed = (
        P(("rep", "shard"), None, None),
        P("shard"),
        P("shard"),
        P("shard", None),
        P("shard"),
        P("shard", None),
        P("shard", None),
        P("shard"),
        P("shard", None),
        P("shard"),
        P("shard"),
        P("shard"),
        P("shard", None),
        P("shard"),
        P("shard", None),
        P("shard"),
        P(("rep", "shard"), None, None),
    )
    return jax.shard_map(
        on_device,
        mesh=mesh,
        in_specs=placed,
        out_specs=(
            P(("rep", "shard"), None, None),
            P(("rep", "shard"), None, None),
            P("shard"),
            P("shard"),
            P("shard", None),
            P("shard"),
            P("shard", None),
            P("shard", None),
            P("shard"),
            P("shard", None),
            P("shard"),
            P("shard"),
            P("shard"),
            P("shard", None),
            P("shard"),
            P("shard", None),
            P("shard"),
        ),
        check_vma=False,
    )
```

```python
import functools

import jax
import jax.numpy as jnp
from jax import lax
from jax.experimental import pallas as pl
from jax.experimental.pallas import tpu as pltpu
from jax.sharding import PartitionSpec as P

HD = 64


EPS = 1e-05
ROOT_HALF = 0.7071067811865476
INV_ROOT_TWO_PI = 0.3989422804014327


def layer_norm(tokens, norm_gain, norm_shift):
    average = jnp.mean(tokens, axis=-1, keepdims=True)
    centered = tokens - average
    inv_std = lax.rsqrt(jnp.mean(centered * centered, axis=-1, keepdims=True) + EPS)
    normed = centered * inv_std
    shaped = normed * norm_gain.astype(jnp.float32) + norm_shift.astype(jnp.float32)
    return (normed, inv_std, shaped.astype(jnp.bfloat16))


def norm_grad(upstream, normed, inv_std, norm_gain):
    scaled = upstream * norm_gain.astype(jnp.float32)
    inner = (
        scaled
        - jnp.mean(scaled, axis=-1, keepdims=True)
        - normed * jnp.mean(scaled * normed, axis=-1, keepdims=True)
    )
    return (inner * inv_std, jnp.sum(upstream * normed, axis=0), jnp.sum(upstream, axis=0))


def matmul(left, right):
    return jnp.dot(left, right, preferred_element_type=jnp.float32)


def times_transposed(left, right):
    return lax.dot_general(
        left, right, (((1,), (1,)), ((), ())), preferred_element_type=jnp.float32
    )


def token_sum(left, right):
    return lax.dot_general(
        left, right, (((0,), (0,)), ((), ())), preferred_element_type=jnp.float32
    )


def gelu_parts(before):
    normal_cdf = 0.5 * (1.0 + lax.erf(before * ROOT_HALF))
    return (
        before * normal_cdf,
        normal_cdf + before * INV_ROOT_TWO_PI * jnp.exp(-0.5 * before * before),
    )


def attend(query, keys, values):
    factor = query.shape[-1] ** (-0.5)
    scores = jnp.einsum("clhd,cmhd->chlm", query, keys, preferred_element_type=jnp.float32) * factor
    row_top = jnp.max(scores, axis=-1, keepdims=True)
    log_total = row_top + jnp.log(jnp.sum(jnp.exp(scores - row_top), axis=-1, keepdims=True))
    weights = jnp.exp(scores - log_total).astype(jnp.bfloat16)
    mixed = jnp.einsum(
        "chlm,cmhd->clhd", weights, values, preferred_element_type=jnp.float32
    ).astype(jnp.bfloat16)
    return (mixed, log_total)


def attend_grad(query, keys, values, mixed, log_total, grad_mixed):
    factor = query.shape[-1] ** (-0.5)
    scores = jnp.einsum("clhd,cmhd->chlm", query, keys, preferred_element_type=jnp.float32) * factor
    weights = jnp.exp(scores - log_total)
    weights_low = weights.astype(jnp.bfloat16)
    grad_values = jnp.einsum(
        "chlm,clhd->cmhd", weights_low, grad_mixed, preferred_element_type=jnp.float32
    )
    grad_weights = jnp.einsum(
        "clhd,cmhd->chlm", grad_mixed, values, preferred_element_type=jnp.float32
    )
    delta = jnp.sum(grad_mixed.astype(jnp.float32) * mixed.astype(jnp.float32), axis=-1)
    delta = jnp.transpose(delta, (0, 2, 1))[..., None]
    grad_scores = (weights * (grad_weights - delta)).astype(jnp.bfloat16)
    grad_query = (
        jnp.einsum("chlm,cmhd->clhd", grad_scores, keys, preferred_element_type=jnp.float32)
        * factor
    )
    grad_keys = (
        jnp.einsum("chlm,clhd->cmhd", grad_scores, query, preferred_element_type=jnp.float32)
        * factor
    )
    return (grad_query, grad_keys, grad_values)


MESH = pl.DeviceIdType.MESH


def ring_place(index, count):
    odd = index % 2
    return (index // 2) * (1 - odd) + (count - 1 - index // 2) * odd


def ring_index(place, count):
    late = place // (count // 2)
    return 2 * place * (1 - late) + (2 * (count - 1 - place) + 1) * late


def ring_steps(stream, count):
    forward = count // 2 if stream % 2 == 0 else count - 1 - count // 2
    return (forward, count - 1 - forward)


def greet(peers):
    barrier = pltpu.get_barrier_semaphore()
    for peer in peers:
        pl.semaphore_signal(barrier, inc=1, device_id=peer, device_id_type=MESH)
    pl.semaphore_wait(barrier, len(peers))


def remote(src, dst, send_sem, recv_sem, peer):
    return pltpu.make_async_remote_copy(
        src_ref=src,
        dst_ref=dst,
        send_sem=send_sem,
        recv_sem=recv_sem,
        device_id=peer,
        device_id_type=MESH,
    )


def gather_kernel(count, streams, *refs):
    own = refs[:streams]
    whole = refs[streams : 2 * streams]
    ring_send, ring_recv, pair_send, pair_recv, local_sem = refs[2 * streams :]
    me = lax.axis_index("shard")
    rep = lax.axis_index("rep")
    core = rep % 2
    place = ring_place(me, count)
    ways = (
        {"shard": ring_index((place + 1) % count, count)},
        {"shard": ring_index((place + count - 1) % count, count)},
    )
    partner = {"rep": rep + 1 - 2 * core}
    greet((*ways, partner))

    def owner_from(way, step):
        offset = count - step if way == 0 else step
        return ring_index((place + offset) % count, count)

    pending = []
    locals_ = []
    hops = {}
    longest = max(max(ring_steps(i, count)) for i in range(streams))
    for step in range(longest + 1):
        for i in range(streams):
            steps = ring_steps(i, count)
            for way in range(2):
                if step > steps[way]:
                    continue
                slot = way * steps[0] + step
                if step > 0:
                    hops[(i, way)].wait_recv()
                    owner = owner_from(way, step)
                    landed = whole[i].at[owner, core]
                    cross = remote(
                        landed, landed, pair_send.at[i, slot - 1], pair_recv.at[i, slot - 1], partner
                    )
                if step < steps[way]:
                    owner = owner_from(way, step)
                    source = own[i].at[core] if step == 0 else whole[i].at[owner, core]
                    hop = remote(
                        source,
                        whole[i].at[owner, core],
                        ring_send.at[i, slot],
                        ring_recv.at[i, slot],
                        ways[way],
                    )
                    hop.start()
                    hops[(i, way)] = hop
                    pending.append(hop)
                if step > 0:
                    cross.start()
                    locals_.append(cross)
        if step == 0:
            keep = [
                pltpu.make_async_copy(own[i], whole[i].at[me], local_sem.at[i])
                for i in range(streams)
            ]
            for copy in keep:
                copy.start()
    for cross in locals_:
        cross.wait()
    for hop in pending:
        hop.wait_send()
    for copy in keep:
        copy.wait()


def gather_all(blocks):
    count = lax.axis_size("shard")
    streams = len(blocks)
    halves = [block.reshape(2, -1, block.shape[-1]) for block in blocks]
    dma = pltpu.SemaphoreType.DMA
    outs = pl.pallas_call(
        functools.partial(gather_kernel, count, streams),
        out_shape=[jax.ShapeDtypeStruct((count, *half.shape), half.dtype) for half in halves],
        in_specs=[pl.BlockSpec(memory_space=pltpu.VMEM)] * streams,
        out_specs=[pl.BlockSpec(memory_space=pl.ANY)] * streams,
        scratch_shapes=[dma((streams, count - 1))] * 4 + [dma((streams,))],
        compiler_params=pltpu.CompilerParams(collective_id=0, has_side_effects=True),
    )(*halves)
    return [out.reshape(-1, out.shape[-1]) for out in outs]


def reduce_kernel(count, peer_bits, streams, *refs):
    term = refs[:streams]
    total = refs[streams : 2 * streams]
    pair_got = refs[2 * streams : 3 * streams]
    ring_out = refs[3 * streams : 4 * streams]
    ring_got = refs[4 * streams : 5 * streams]
    rep_out = refs[5 * streams : 6 * streams]
    rep_got = refs[6 * streams : 7 * streams]
    (
        pair_send,
        pair_recv,
        ring_send,
        ring_recv,
        rep_send,
        rep_recv,
        last_send,
        last_recv,
    ) = refs[7 * streams :]
    me = lax.axis_index("shard")
    rep = lax.axis_index("rep")
    core = rep % 2
    place = ring_place(me, count)
    ways = (
        {"shard": ring_index((place + 1) % count, count)},
        {"shard": ring_index((place + count - 1) % count, count)},
    )
    partner = {"rep": rep + 1 - 2 * core}
    across = [
        {"rep": rep + bit * (1 - 2 * ((rep // bit) % 2))} for bit in peer_bits
    ]
    greet((*ways, partner, *across))

    def target(way, steps, step):
        reach = steps[way] - step
        return ring_index((place + (reach if way == 0 else count - reach)) % count, count)

    sent = []
    crossed = {}
    longest = max(max(ring_steps(i, count)) for i in range(streams))
    for step in range(longest + 1):
        for i in range(streams):
            steps = ring_steps(i, count)
            for way in range(2):
                if step < steps[way]:
                    owner, slot = target(way, steps, step), way * steps[0] + step
                elif step == steps[0] and way == 0:
                    owner, slot = me, count - 1
                else:
                    continue
                cross = remote(
                    term[i].at[owner, 1 - core],
                    pair_got[i].at[owner],
                    pair_send.at[i, slot],
                    pair_recv.at[i, slot],
                    partner,
                )
                cross.start()
                crossed[(i, slot)] = cross
                sent.append(cross)

    def pair_sum(i, owner, slot):
        crossed[(i, slot)].wait_recv()
        return term[i][owner, core].astype(jnp.float32) + pair_got[i][owner].astype(jnp.float32)

    hops = {}
    for step in range(longest):
        for i in range(streams):
            steps = ring_steps(i, count)
            for way in range(2):
                if step >= steps[way]:
                    continue
                slot = way * steps[0] + step
                partial = pair_sum(i, target(way, steps, step), slot)
                if step > 0:
                    hops[(i, way)].wait_recv()
                    partial += ring_got[i][slot - 1].astype(jnp.float32)
                ring_out[i][slot] = partial.astype(ring_out[i].dtype)
                hop = remote(
                    ring_out[i].at[slot],
                    ring_got[i].at[slot],
                    ring_send.at[i, slot],
                    ring_recv.at[i, slot],
                    ways[way],
                )
                hop.start()
                hops[(i, way)] = hop
                sent.append(hop)
    owned = {}
    swaps = {}

    def swap(i, level):
        rep_out[i][level] = owned[i].astype(rep_out[i].dtype)
        move = remote(
            rep_out[i].at[level],
            rep_got[i].at[level],
            rep_send.at[i, level],
            rep_recv.at[i, level],
            across[level],
        )
        move.start()
        swaps[(i, level)] = move
        sent.append(move)

    for i in range(streams):
        steps = ring_steps(i, count)
        value = pair_sum(i, me, count - 1)
        for way in range(2):
            if steps[way]:
                hops[(i, way)].wait_recv()
                value += ring_got[i][way * steps[0] + steps[way] - 1].astype(jnp.float32)
        owned[i] = value
        if across:
            swap(i, 0)
    for level in range(len(across)):
        for i in range(streams):
            swaps[(i, level)].wait_recv()
            owned[i] = rep_out[i][level].astype(jnp.float32) + rep_got[i][level].astype(jnp.float32)
            if level + 1 < len(across):
                swap(i, level + 1)
            else:
                total[i][core] = owned[i]
                final = remote(
                    total[i].at[core],
                    total[i].at[core],
                    last_send.at[i],
                    last_recv.at[i],
                    partner,
                )
                final.start()
                crossed[(i, "final")] = final
    for i in range(streams):
        crossed[(i, "final")].wait()
    for copy in sent:
        copy.wait_send()


def reduce_all(terms):
    count = lax.axis_size("shard")
    reps = lax.axis_size("rep")
    peer_bits = [1 << k for k in range(1, reps.bit_length() - 1)]
    streams = len(terms)
    halves = [term.reshape(count, 2, -1, term.shape[-1]) for term in terms]
    dma = pltpu.SemaphoreType.DMA

    def slots(number):
        return [pltpu.VMEM((number, *half.shape[2:]), half.dtype) for half in halves]

    levels = len(peer_bits)
    outs = pl.pallas_call(
        functools.partial(reduce_kernel, count, peer_bits, streams),
        out_shape=[jax.ShapeDtypeStruct(half.shape[1:], jnp.float32) for half in halves],
        in_specs=[pl.BlockSpec(memory_space=pltpu.VMEM)] * streams,
        out_specs=[pl.BlockSpec(memory_space=pltpu.VMEM)] * streams,
        scratch_shapes=slots(count)
        + slots(count - 1)
        + slots(count - 1)
        + slots(levels)
        + slots(levels)
        + [dma((streams, count))] * 2
        + [dma((streams, count - 1))] * 2
        + [dma((streams, levels))] * 2
        + [dma((streams,))] * 2,
        compiler_params=pltpu.CompilerParams(
            collective_id=1, has_side_effects=True, vmem_limit_bytes=60 * 1024 * 1024
        ),
    )(*halves)
    return [out.reshape(-1, out.shape[-1]) for out in outs]


def cut_columns(matrix, likes, flat=True):
    pieces = []
    start = 0
    for like in likes:
        width = like.shape[-1]
        piece = matrix[:, start : start + width]
        pieces.append(piece.reshape(-1) if flat else piece)
        start += width
    return tuple(pieces)


def on_device(
    block_input,
    attn_gain,
    attn_shift,
    query_weight,
    query_bias,
    key_weight,
    value_weight,
    value_bias,
    out_weight,
    out_bias,
    mlp_gain,
    mlp_shift,
    hidden_weight,
    hidden_bias,
    proj_weight,
    proj_bias,
    out_cotangent,
):
    clip_count, frame_count, model_width = block_input.shape
    head_count = model_width // HD
    token_count = clip_count * frame_count

    def split_heads(matrix):
        return matrix.reshape(clip_count, frame_count, head_count, HD)

    def join_heads(tensor):
        return tensor.reshape(token_count, model_width)

    residual = block_input.reshape(token_count, model_width)
    vectors = (
        attn_gain,
        attn_shift,
        query_bias,
        value_bias,
        out_bias,
        mlp_gain,
        mlp_shift,
        proj_bias,
        hidden_bias,
    )
    squares = (query_weight, key_weight, value_weight, out_weight)
    squares_all, hidden_all, proj_all, vectors_all = gather_all(
        (
            jnp.concatenate(squares, axis=1),
            hidden_weight,
            proj_weight,
            jnp.concatenate(vectors).reshape(2, -1),
        )
    )
    vectors_all = vectors_all.reshape(lax.axis_size("shard"), -1)
    (
        attn_gain_all,
        attn_shift_all,
        query_bias_all,
        value_bias_all,
        out_bias_all,
        mlp_gain_all,
        mlp_shift_all,
        proj_bias_all,
        hidden_bias_all,
    ) = cut_columns(vectors_all, vectors)
    query_all, key_all, value_all, out_all = cut_columns(squares_all, squares, False)
    normed_one, inv_one, input_low = layer_norm(residual, attn_gain_all, attn_shift_all)
    query_low = (matmul(input_low, query_all) + query_bias_all.astype(jnp.float32)).astype(
        jnp.bfloat16
    )
    keys_low = matmul(input_low, key_all).astype(jnp.bfloat16)
    values_low = (matmul(input_low, value_all) + value_bias_all.astype(jnp.float32)).astype(
        jnp.bfloat16
    )
    mixed, log_total = attend(
        split_heads(query_low), split_heads(keys_low), split_heads(values_low)
    )
    mixed_rows = join_heads(mixed)
    middle = residual + matmul(mixed_rows, out_all) + out_bias_all.astype(jnp.float32)
    normed_two, inv_two, middle_low = layer_norm(middle, mlp_gain_all, mlp_shift_all)
    before_act = matmul(middle_low, hidden_all) + hidden_bias_all.astype(jnp.float32)
    activated, slope = gelu_parts(before_act)
    act_low = activated.astype(jnp.bfloat16)
    block_output = middle + matmul(act_low, proj_all) + proj_bias_all.astype(jnp.float32)
    upstream = out_cotangent.reshape(token_count, model_width)
    up_low = upstream.astype(jnp.bfloat16)
    proj_term = token_sum(act_low, up_low)
    proj_bias_term = jnp.sum(upstream, axis=0)
    grad_before = times_transposed(up_low, proj_all) * slope
    before_low = grad_before.astype(jnp.bfloat16)
    hidden_term = token_sum(middle_low, before_low)
    hidden_bias_term = jnp.sum(grad_before, axis=0)
    grad_normed_two = times_transposed(before_low, hidden_all)
    grad_middle_norm, mlp_gain_term, mlp_shift_term = norm_grad(
        grad_normed_two, normed_two, inv_two, mlp_gain_all
    )
    grad_middle = upstream + grad_middle_norm
    middle_grad_low = grad_middle.astype(jnp.bfloat16)
    out_term = token_sum(mixed_rows, middle_grad_low)
    out_bias_term = jnp.sum(grad_middle, axis=0)
    grad_mixed = times_transposed(middle_grad_low, out_all).astype(jnp.bfloat16)
    grad_query, grad_keys, grad_values = attend_grad(
        split_heads(query_low),
        split_heads(keys_low),
        split_heads(values_low),
        mixed,
        log_total,
        split_heads(grad_mixed),
    )
    grad_query = join_heads(grad_query)
    grad_keys = join_heads(grad_keys)
    grad_values = join_heads(grad_values)
    query_bias_term = jnp.sum(grad_query, axis=0)
    value_bias_term = jnp.sum(grad_values, axis=0)
    query_grad_low = grad_query.astype(jnp.bfloat16)
    key_grad_low = grad_keys.astype(jnp.bfloat16)
    value_grad_low = grad_values.astype(jnp.bfloat16)
    query_term = token_sum(input_low, query_grad_low)
    key_term = token_sum(input_low, key_grad_low)
    value_term = token_sum(input_low, value_grad_low)
    grad_normed_one = (
        times_transposed(query_grad_low, query_all)
        + times_transposed(key_grad_low, key_all)
        + times_transposed(value_grad_low, value_all)
    )
    grad_input_norm, attn_gain_term, attn_shift_term = norm_grad(
        grad_normed_one, normed_one, inv_one, attn_gain_all
    )
    input_grad = grad_middle + grad_input_norm
    shards = lax.axis_size("shard")
    vector_terms = jnp.concatenate(
        [
            term.reshape(shards, -1)
            for term in (
                attn_gain_term,
                attn_shift_term,
                query_bias_term,
                value_bias_term,
                out_bias_term,
                mlp_gain_term,
                mlp_shift_term,
                proj_bias_term,
                hidden_bias_term,
            )
        ],
        axis=1,
    )
    square_terms = jnp.concatenate(
        [
            term.astype(jnp.bfloat16)
            for term in (query_term, key_term, value_term, out_term)
        ],
        axis=1,
    )
    square_owned, hidden_weight_grad, proj_weight_grad, vector_owned = reduce_all(
        (
            square_terms,
            hidden_term.astype(jnp.bfloat16),
            proj_term.astype(jnp.bfloat16),
            vector_terms.reshape(2 * shards, -1),
        )
    )
    (
        attn_gain_grad,
        attn_shift_grad,
        query_bias_grad,
        value_bias_grad,
        out_bias_grad,
        mlp_gain_grad,
        mlp_shift_grad,
        proj_bias_grad,
        hidden_bias_grad,
    ) = cut_columns(vector_owned.reshape(1, -1), vectors)
    (
        query_weight_grad,
        key_weight_grad,
        value_weight_grad,
        out_weight_grad,
    ) = cut_columns(square_owned, squares, False)
    return (
        block_output.reshape(clip_count, frame_count, model_width),
        input_grad.reshape(clip_count, frame_count, model_width),
        attn_gain_grad,
        attn_shift_grad,
        query_weight_grad,
        query_bias_grad,
        key_weight_grad,
        value_weight_grad,
        value_bias_grad,
        out_weight_grad,
        out_bias_grad,
        mlp_gain_grad,
        mlp_shift_grad,
        hidden_weight_grad,
        hidden_bias_grad,
        proj_weight_grad,
        proj_bias_grad,
    )


def solution(mesh):
    placed = (
        P(("rep", "shard"), None, None),
        P("shard"),
        P("shard"),
        P("shard", None),
        P("shard"),
        P("shard", None),
        P("shard", None),
        P("shard"),
        P("shard", None),
        P("shard"),
        P("shard"),
        P("shard"),
        P("shard", None),
        P("shard"),
        P("shard", None),
        P("shard"),
        P(("rep", "shard"), None, None),
    )
    return jax.shard_map(
        on_device,
        mesh=mesh,
        in_specs=placed,
        out_specs=(
            P(("rep", "shard"), None, None),
            P(("rep", "shard"), None, None),
            P("shard"),
            P("shard"),
            P("shard", None),
            P("shard"),
            P("shard", None),
            P("shard", None),
            P("shard"),
            P("shard", None),
            P("shard"),
            P("shard"),
            P("shard"),
            P("shard", None),
            P("shard"),
            P("shard", None),
            P("shard"),
        ),
        check_vma=False,
    )
```

```python
import functools

import jax
import jax.numpy as jnp
from jax import lax
from jax.experimental import pallas as pl
from jax.experimental.pallas import tpu as pltpu
from jax.sharding import PartitionSpec as P

HD = 64


EPS = 1e-05
ROOT_HALF = 0.7071067811865476
INV_ROOT_TWO_PI = 0.3989422804014327


def layer_norm(tokens, norm_gain, norm_shift):
    average = jnp.mean(tokens, axis=-1, keepdims=True)
    centered = tokens - average
    inv_std = lax.rsqrt(jnp.mean(centered * centered, axis=-1, keepdims=True) + EPS)
    normed = centered * inv_std
    shaped = normed * norm_gain.astype(jnp.float32) + norm_shift.astype(jnp.float32)
    return (normed, inv_std, shaped.astype(jnp.bfloat16))


def norm_grad(upstream, normed, inv_std, norm_gain):
    scaled = upstream * norm_gain.astype(jnp.float32)
    inner = (
        scaled
        - jnp.mean(scaled, axis=-1, keepdims=True)
        - normed * jnp.mean(scaled * normed, axis=-1, keepdims=True)
    )
    return (inner * inv_std, jnp.sum(upstream * normed, axis=0), jnp.sum(upstream, axis=0))


def matmul(left, right):
    return jnp.dot(left, right, preferred_element_type=jnp.float32)


def times_transposed(left, right):
    return lax.dot_general(
        left, right, (((1,), (1,)), ((), ())), preferred_element_type=jnp.float32
    )


def token_sum(left, right):
    return lax.dot_general(
        left, right, (((0,), (0,)), ((), ())), preferred_element_type=jnp.float32
    )


def gelu_parts(before):
    normal_cdf = 0.5 * (1.0 + lax.erf(before * ROOT_HALF))
    return (
        before * normal_cdf,
        normal_cdf + before * INV_ROOT_TWO_PI * jnp.exp(-0.5 * before * before),
    )


def attend(query, keys, values):
    factor = query.shape[-1] ** (-0.5)
    scores = jnp.einsum("clhd,cmhd->chlm", query, keys, preferred_element_type=jnp.float32) * factor
    row_top = jnp.max(scores, axis=-1, keepdims=True)
    log_total = row_top + jnp.log(jnp.sum(jnp.exp(scores - row_top), axis=-1, keepdims=True))
    weights = jnp.exp(scores - log_total).astype(jnp.bfloat16)
    mixed = jnp.einsum(
        "chlm,cmhd->clhd", weights, values, preferred_element_type=jnp.float32
    ).astype(jnp.bfloat16)
    return (mixed, log_total)


def attend_grad(query, keys, values, mixed, log_total, grad_mixed):
    factor = query.shape[-1] ** (-0.5)
    scores = jnp.einsum("clhd,cmhd->chlm", query, keys, preferred_element_type=jnp.float32) * factor
    weights = jnp.exp(scores - log_total)
    weights_low = weights.astype(jnp.bfloat16)
    grad_values = jnp.einsum(
        "chlm,clhd->cmhd", weights_low, grad_mixed, preferred_element_type=jnp.float32
    )
    grad_weights = jnp.einsum(
        "clhd,cmhd->chlm", grad_mixed, values, preferred_element_type=jnp.float32
    )
    delta = jnp.sum(grad_mixed.astype(jnp.float32) * mixed.astype(jnp.float32), axis=-1)
    delta = jnp.transpose(delta, (0, 2, 1))[..., None]
    grad_scores = (weights * (grad_weights - delta)).astype(jnp.bfloat16)
    grad_query = (
        jnp.einsum("chlm,cmhd->clhd", grad_scores, keys, preferred_element_type=jnp.float32)
        * factor
    )
    grad_keys = (
        jnp.einsum("chlm,clhd->cmhd", grad_scores, query, preferred_element_type=jnp.float32)
        * factor
    )
    return (grad_query, grad_keys, grad_values)


MESH = pl.DeviceIdType.MESH


def ring_place(index, count):
    odd = index % 2
    return (index // 2) * (1 - odd) + (count - 1 - index // 2) * odd


def ring_index(place, count):
    late = place // (count // 2)
    return 2 * place * (1 - late) + (2 * (count - 1 - place) + 1) * late


def ring_steps(stream, count):
    forward = count // 2 if stream % 2 == 0 else count - 1 - count // 2
    return (forward, count - 1 - forward)


def greet(peers):
    barrier = pltpu.get_barrier_semaphore()
    for peer in peers:
        pl.semaphore_signal(barrier, inc=1, device_id=peer, device_id_type=MESH)
    pl.semaphore_wait(barrier, len(peers))


def remote(src, dst, send_sem, recv_sem, peer):
    return pltpu.make_async_remote_copy(
        src_ref=src,
        dst_ref=dst,
        send_sem=send_sem,
        recv_sem=recv_sem,
        device_id=peer,
        device_id_type=MESH,
    )


def gather_kernel(count, streams, *refs):
    own = refs[:streams]
    whole = refs[streams : 2 * streams]
    (
        ring_send,
        ring_recv,
        pair_send,
        pair_recv,
        side_send,
        side_recv,
        late_send,
        late_recv,
        local_sem,
    ) = refs[2 * streams :]
    me = lax.axis_index("shard")
    rep = lax.axis_index("rep")
    core = rep % 2
    place = ring_place(me, count)
    ways = (
        {"shard": ring_index((place + 1) % count, count)},
        {"shard": ring_index((place + count - 1) % count, count)},
    )
    partner = {"rep": rep + 1 - 2 * core}
    side = (rep // 2) % 2
    across = {"rep": rep + 2 * (1 - 2 * side)}
    greet((*ways, partner, across))

    def columns(i):
        width = own[i].shape[-1]
        if width % 384:
            return (pl.ds(0, width), None, None)
        third = width // 3
        mine = pl.ds(pl.multiple_of(side * third, 128), 2 * third)
        give = pl.ds(pl.multiple_of(2 * side * third, 128), third)
        take = pl.ds(pl.multiple_of(2 * (1 - side) * third, 128), third)
        return (mine, give, take)

    shares = [columns(i) for i in range(streams)]
    sides = {}

    def pass_on(i, way, step):
        slot = way * ring_steps(i, count)[0] + step - 1
        take = shares[i][2]
        sides[(i, slot)].wait_recv()
        landed = whole[i].at[owner_from(way, step), core, :, take]
        late = remote(landed, landed, late_send.at[i, slot], late_recv.at[i, slot], partner)
        late.start()
        locals_.append(late)

    def owner_from(way, step):
        offset = count - step if way == 0 else step
        return ring_index((place + offset) % count, count)

    pending = []
    locals_ = []
    hops = {}
    longest = max(max(ring_steps(i, count)) for i in range(streams))
    for step in range(longest + 1):
        for i in range(streams):
            steps = ring_steps(i, count)
            for way in range(2):
                if step > steps[way]:
                    continue
                slot = way * steps[0] + step
                if step > 0:
                    hops[(i, way)].wait_recv()
                    owner = owner_from(way, step)
                    landed = whole[i].at[owner, core, :, shares[i][0]]
                    cross = remote(
                        landed, landed, pair_send.at[i, slot - 1], pair_recv.at[i, slot - 1], partner
                    )
                if step < steps[way]:
                    owner = owner_from(way, step)
                    into = whole[i].at[owner, core, :, shares[i][0]]
                    source = own[i].at[core, :, shares[i][0]] if step == 0 else into
                    hop = remote(
                        source,
                        into,
                        ring_send.at[i, slot],
                        ring_recv.at[i, slot],
                        ways[way],
                    )
                    hop.start()
                    hops[(i, way)] = hop
                    pending.append(hop)
                if step > 0:
                    if shares[i][1] is not None:
                        given = whole[i].at[owner_from(way, step), core, :, shares[i][1]]
                        aside = remote(
                            given,
                            given,
                            side_send.at[i, slot - 1],
                            side_recv.at[i, slot - 1],
                            across,
                        )
                        aside.start()
                        sides[(i, slot - 1)] = aside
                        pending.append(aside)
                    cross.start()
                    locals_.append(cross)
                if step > 1 and shares[i][1] is not None:
                    pass_on(i, way, step - 1)
        if step == 0:
            keep = [
                pltpu.make_async_copy(own[i], whole[i].at[me], local_sem.at[i])
                for i in range(streams)
            ]
            for copy in keep:
                copy.start()
    for i in range(streams):
        for way in range(2):
            if shares[i][1] is not None:
                pass_on(i, way, ring_steps(i, count)[way])
    for cross in locals_:
        cross.wait()
    for hop in pending:
        hop.wait_send()
    for copy in keep:
        copy.wait()


def gather_all(blocks):
    count = lax.axis_size("shard")
    streams = len(blocks)
    halves = [block.reshape(2, -1, block.shape[-1]) for block in blocks]
    dma = pltpu.SemaphoreType.DMA
    outs = pl.pallas_call(
        functools.partial(gather_kernel, count, streams),
        out_shape=[jax.ShapeDtypeStruct((count, *half.shape), half.dtype) for half in halves],
        in_specs=[pl.BlockSpec(memory_space=pltpu.VMEM)] * streams,
        out_specs=[pl.BlockSpec(memory_space=pl.ANY)] * streams,
        scratch_shapes=[dma((streams, count - 1))] * 8 + [dma((streams,))],
        compiler_params=pltpu.CompilerParams(collective_id=0, has_side_effects=True),
    )(*halves)
    return [out.reshape(-1, out.shape[-1]) for out in outs]


def reduce_kernel(count, peer_bits, streams, *refs):
    term = refs[:streams]
    total = refs[streams : 2 * streams]
    pair_got = refs[2 * streams : 3 * streams]
    ring_out = refs[3 * streams : 4 * streams]
    ring_got = refs[4 * streams : 5 * streams]
    rep_out = refs[5 * streams : 6 * streams]
    rep_got = refs[6 * streams : 7 * streams]
    (
        pair_send,
        pair_recv,
        ring_send,
        ring_recv,
        rep_send,
        rep_recv,
        last_send,
        last_recv,
    ) = refs[7 * streams :]
    me = lax.axis_index("shard")
    rep = lax.axis_index("rep")
    core = rep % 2
    place = ring_place(me, count)
    ways = (
        {"shard": ring_index((place + 1) % count, count)},
        {"shard": ring_index((place + count - 1) % count, count)},
    )
    partner = {"rep": rep + 1 - 2 * core}
    across = [
        {"rep": rep + bit * (1 - 2 * ((rep // bit) % 2))} for bit in peer_bits
    ]
    greet((*ways, partner, *across))

    def target(way, steps, step):
        reach = steps[way] - step
        return ring_index((place + (reach if way == 0 else count - reach)) % count, count)

    sent = []
    crossed = {}
    longest = max(max(ring_steps(i, count)) for i in range(streams))
    for step in range(longest + 1):
        for i in range(streams):
            steps = ring_steps(i, count)
            for way in range(2):
                if step < steps[way]:
                    owner, slot = target(way, steps, step), way * steps[0] + step
                elif step == steps[0] and way == 0:
                    owner, slot = me, count - 1
                else:
                    continue
                cross = remote(
                    term[i].at[owner, 1 - core],
                    pair_got[i].at[owner],
                    pair_send.at[i, slot],
                    pair_recv.at[i, slot],
                    partner,
                )
                cross.start()
                crossed[(i, slot)] = cross
                sent.append(cross)

    def pair_sum(i, owner, slot):
        crossed[(i, slot)].wait_recv()
        return term[i][owner, core].astype(jnp.float32) + pair_got[i][owner].astype(jnp.float32)

    hops = {}
    for step in range(longest):
        for i in range(streams):
            steps = ring_steps(i, count)
            for way in range(2):
                if step >= steps[way]:
                    continue
                slot = way * steps[0] + step
                partial = pair_sum(i, target(way, steps, step), slot)
                if step > 0:
                    hops[(i, way)].wait_recv()
                    partial += ring_got[i][slot - 1].astype(jnp.float32)
                ring_out[i][slot] = partial.astype(ring_out[i].dtype)
                hop = remote(
                    ring_out[i].at[slot],
                    ring_got[i].at[slot],
                    ring_send.at[i, slot],
                    ring_recv.at[i, slot],
                    ways[way],
                )
                hop.start()
                hops[(i, way)] = hop
                sent.append(hop)
    owned = {}
    swaps = {}

    def swap(i, level):
        rep_out[i][level] = owned[i].astype(rep_out[i].dtype)
        move = remote(
            rep_out[i].at[level],
            rep_got[i].at[level],
            rep_send.at[i, level],
            rep_recv.at[i, level],
            across[level],
        )
        move.start()
        swaps[(i, level)] = move
        sent.append(move)

    for i in range(streams):
        steps = ring_steps(i, count)
        value = pair_sum(i, me, count - 1)
        for way in range(2):
            if steps[way]:
                hops[(i, way)].wait_recv()
                value += ring_got[i][way * steps[0] + steps[way] - 1].astype(jnp.float32)
        owned[i] = value
        if across:
            swap(i, 0)
    for level in range(len(across)):
        for i in range(streams):
            swaps[(i, level)].wait_recv()
            owned[i] = rep_out[i][level].astype(jnp.float32) + rep_got[i][level].astype(jnp.float32)
            if level + 1 < len(across):
                swap(i, level + 1)
            else:
                total[i][core] = owned[i]
                final = remote(
                    total[i].at[core],
                    total[i].at[core],
                    last_send.at[i],
                    last_recv.at[i],
                    partner,
                )
                final.start()
                crossed[(i, "final")] = final
    for i in range(streams):
        crossed[(i, "final")].wait()
    for copy in sent:
        copy.wait_send()


def reduce_all(terms):
    count = lax.axis_size("shard")
    reps = lax.axis_size("rep")
    peer_bits = [1 << k for k in range(1, reps.bit_length() - 1)]
    streams = len(terms)
    halves = [term.reshape(count, 2, -1, term.shape[-1]) for term in terms]
    dma = pltpu.SemaphoreType.DMA

    def slots(number):
        return [pltpu.VMEM((number, *half.shape[2:]), half.dtype) for half in halves]

    levels = len(peer_bits)
    outs = pl.pallas_call(
        functools.partial(reduce_kernel, count, peer_bits, streams),
        out_shape=[jax.ShapeDtypeStruct(half.shape[1:], jnp.float32) for half in halves],
        in_specs=[pl.BlockSpec(memory_space=pltpu.VMEM)] * streams,
        out_specs=[pl.BlockSpec(memory_space=pltpu.VMEM)] * streams,
        scratch_shapes=slots(count)
        + slots(count - 1)
        + slots(count - 1)
        + slots(levels)
        + slots(levels)
        + [dma((streams, count))] * 2
        + [dma((streams, count - 1))] * 2
        + [dma((streams, levels))] * 2
        + [dma((streams,))] * 2,
        compiler_params=pltpu.CompilerParams(
            collective_id=1, has_side_effects=True, vmem_limit_bytes=60 * 1024 * 1024
        ),
    )(*halves)
    return [out.reshape(-1, out.shape[-1]) for out in outs]


def cut_columns(matrix, likes, flat=True):
    pieces = []
    start = 0
    for like in likes:
        width = like.shape[-1]
        piece = matrix[:, start : start + width]
        pieces.append(piece.reshape(-1) if flat else piece)
        start += width
    return tuple(pieces)


def on_device(
    block_input,
    attn_gain,
    attn_shift,
    query_weight,
    query_bias,
    key_weight,
    value_weight,
    value_bias,
    out_weight,
    out_bias,
    mlp_gain,
    mlp_shift,
    hidden_weight,
    hidden_bias,
    proj_weight,
    proj_bias,
    out_cotangent,
):
    clip_count, frame_count, model_width = block_input.shape
    head_count = model_width // HD
    token_count = clip_count * frame_count

    def split_heads(matrix):
        return matrix.reshape(clip_count, frame_count, head_count, HD)

    def join_heads(tensor):
        return tensor.reshape(token_count, model_width)

    residual = block_input.reshape(token_count, model_width)
    vectors = (
        attn_gain,
        attn_shift,
        query_bias,
        value_bias,
        out_bias,
        mlp_gain,
        mlp_shift,
        proj_bias,
        hidden_bias,
    )
    squares = (query_weight, key_weight, value_weight, out_weight)
    squares_all, hidden_all, proj_all, vectors_all = gather_all(
        (
            jnp.concatenate(squares, axis=1),
            hidden_weight,
            proj_weight,
            jnp.concatenate(vectors).reshape(2, -1),
        )
    )
    vectors_all = vectors_all.reshape(lax.axis_size("shard"), -1)
    (
        attn_gain_all,
        attn_shift_all,
        query_bias_all,
        value_bias_all,
        out_bias_all,
        mlp_gain_all,
        mlp_shift_all,
        proj_bias_all,
        hidden_bias_all,
    ) = cut_columns(vectors_all, vectors)
    query_all, key_all, value_all, out_all = cut_columns(squares_all, squares, False)
    normed_one, inv_one, input_low = layer_norm(residual, attn_gain_all, attn_shift_all)
    query_low = (matmul(input_low, query_all) + query_bias_all.astype(jnp.float32)).astype(
        jnp.bfloat16
    )
    keys_low = matmul(input_low, key_all).astype(jnp.bfloat16)
    values_low = (matmul(input_low, value_all) + value_bias_all.astype(jnp.float32)).astype(
        jnp.bfloat16
    )
    mixed, log_total = attend(
        split_heads(query_low), split_heads(keys_low), split_heads(values_low)
    )
    mixed_rows = join_heads(mixed)
    middle = residual + matmul(mixed_rows, out_all) + out_bias_all.astype(jnp.float32)
    normed_two, inv_two, middle_low = layer_norm(middle, mlp_gain_all, mlp_shift_all)
    before_act = matmul(middle_low, hidden_all) + hidden_bias_all.astype(jnp.float32)
    activated, slope = gelu_parts(before_act)
    act_low = activated.astype(jnp.bfloat16)
    block_output = middle + matmul(act_low, proj_all) + proj_bias_all.astype(jnp.float32)
    upstream = out_cotangent.reshape(token_count, model_width)
    up_low = upstream.astype(jnp.bfloat16)
    proj_term = token_sum(act_low, up_low)
    proj_bias_term = jnp.sum(upstream, axis=0)
    grad_before = times_transposed(up_low, proj_all) * slope
    before_low = grad_before.astype(jnp.bfloat16)
    hidden_term = token_sum(middle_low, before_low)
    hidden_bias_term = jnp.sum(grad_before, axis=0)
    grad_normed_two = times_transposed(before_low, hidden_all)
    grad_middle_norm, mlp_gain_term, mlp_shift_term = norm_grad(
        grad_normed_two, normed_two, inv_two, mlp_gain_all
    )
    grad_middle = upstream + grad_middle_norm
    middle_grad_low = grad_middle.astype(jnp.bfloat16)
    out_term = token_sum(mixed_rows, middle_grad_low)
    out_bias_term = jnp.sum(grad_middle, axis=0)
    grad_mixed = times_transposed(middle_grad_low, out_all).astype(jnp.bfloat16)
    grad_query, grad_keys, grad_values = attend_grad(
        split_heads(query_low),
        split_heads(keys_low),
        split_heads(values_low),
        mixed,
        log_total,
        split_heads(grad_mixed),
    )
    grad_query = join_heads(grad_query)
    grad_keys = join_heads(grad_keys)
    grad_values = join_heads(grad_values)
    query_bias_term = jnp.sum(grad_query, axis=0)
    value_bias_term = jnp.sum(grad_values, axis=0)
    query_grad_low = grad_query.astype(jnp.bfloat16)
    key_grad_low = grad_keys.astype(jnp.bfloat16)
    value_grad_low = grad_values.astype(jnp.bfloat16)
    query_term = token_sum(input_low, query_grad_low)
    key_term = token_sum(input_low, key_grad_low)
    value_term = token_sum(input_low, value_grad_low)
    grad_normed_one = (
        times_transposed(query_grad_low, query_all)
        + times_transposed(key_grad_low, key_all)
        + times_transposed(value_grad_low, value_all)
    )
    grad_input_norm, attn_gain_term, attn_shift_term = norm_grad(
        grad_normed_one, normed_one, inv_one, attn_gain_all
    )
    input_grad = grad_middle + grad_input_norm
    shards = lax.axis_size("shard")
    vector_terms = jnp.concatenate(
        [
            term.reshape(shards, -1)
            for term in (
                attn_gain_term,
                attn_shift_term,
                query_bias_term,
                value_bias_term,
                out_bias_term,
                mlp_gain_term,
                mlp_shift_term,
                proj_bias_term,
                hidden_bias_term,
            )
        ],
        axis=1,
    )
    square_terms = jnp.concatenate(
        [
            term.astype(jnp.bfloat16)
            for term in (query_term, key_term, value_term, out_term)
        ],
        axis=1,
    )
    square_owned, hidden_weight_grad, proj_weight_grad, vector_owned = reduce_all(
        (
            square_terms,
            hidden_term.astype(jnp.bfloat16),
            proj_term.astype(jnp.bfloat16),
            vector_terms.reshape(2 * shards, -1),
        )
    )
    (
        attn_gain_grad,
        attn_shift_grad,
        query_bias_grad,
        value_bias_grad,
        out_bias_grad,
        mlp_gain_grad,
        mlp_shift_grad,
        proj_bias_grad,
        hidden_bias_grad,
    ) = cut_columns(vector_owned.reshape(1, -1), vectors)
    (
        query_weight_grad,
        key_weight_grad,
        value_weight_grad,
        out_weight_grad,
    ) = cut_columns(square_owned, squares, False)
    return (
        block_output.reshape(clip_count, frame_count, model_width),
        input_grad.reshape(clip_count, frame_count, model_width),
        attn_gain_grad,
        attn_shift_grad,
        query_weight_grad,
        query_bias_grad,
        key_weight_grad,
        value_weight_grad,
        value_bias_grad,
        out_weight_grad,
        out_bias_grad,
        mlp_gain_grad,
        mlp_shift_grad,
        hidden_weight_grad,
        hidden_bias_grad,
        proj_weight_grad,
        proj_bias_grad,
    )


def solution(mesh):
    placed = (
        P(("rep", "shard"), None, None),
        P("shard"),
        P("shard"),
        P("shard", None),
        P("shard"),
        P("shard", None),
        P("shard", None),
        P("shard"),
        P("shard", None),
        P("shard"),
        P("shard"),
        P("shard"),
        P("shard", None),
        P("shard"),
        P("shard", None),
        P("shard"),
        P(("rep", "shard"), None, None),
    )
    return jax.shard_map(
        on_device,
        mesh=mesh,
        in_specs=placed,
        out_specs=(
            P(("rep", "shard"), None, None),
            P(("rep", "shard"), None, None),
            P("shard"),
            P("shard"),
            P("shard", None),
            P("shard"),
            P("shard", None),
            P("shard", None),
            P("shard"),
            P("shard", None),
            P("shard"),
            P("shard"),
            P("shard"),
            P("shard", None),
            P("shard"),
            P("shard", None),
            P("shard"),
        ),
        check_vma=False,
    )
```
